256 devices in a mesh: rcv: 32 (over z, y), hd: 8 (over x, core).
Axes of the slice: x: 4, y: 4, z: 8, core: 2. Of those that a mesh axis runs over, the one named last changes fastest.
Arguments:
- stream: bfloat16 [32768, 1024], P(('rcv', 'hd')), may hold values from -3 to 3
- queries: bfloat16 [32768, 1024], P(('rcv', 'hd')), may hold values from -9 to 9
- keys: bfloat16 [32768, 1024], P(('rcv', 'hd')), may hold values from -9 to 9
- values: bfloat16 [32768, 1024], P(('rcv', 'hd')), may hold values from -6 to 6
- out_proj: bfloat16 [1024, 1024], replicated, may hold values from -0.375 to 0.375
- norm_gain: float32 [1024], replicated, may hold values from 0.5 to 1.5
- expert_weights: bfloat16 [1024, 64, 3, 512], P(None, 'rcv'), may hold values from -0.1875 to 0.1875
- expert_ids: int32 [32768, 4], P(('rcv', 'hd')), may hold values from 0 to 63, as said below
- gate_weights: float32 [32768, 4], P(('rcv', 'hd')), may hold values from 0.1 to 1
- out_cotangent: bfloat16 [32768, 1024], P(('rcv', 'hd')), may hold values from -6 to 6
Outputs:
- block_out: bfloat16 [32768, 1024], P(('rcv', 'hd'))
- stream_grad: bfloat16 [32768, 1024], P(('rcv', 'hd'))
The draws below stay inside these ranges and needn't reach their ends.
Inputs may be any that keep to these rules, and one draw needn't show every extreme that they name: `expert_ids`: each token names 4 different experts; its k-th id lies in k * 16 to (k + 1) * 16 - 1. Within each aligned block of 128 rows no expert is named more than 10 times, and in each of these 4 ranges one expert, the same for all blocks, is named exactly 10 times in every block.
All inputs are finite; a program needn't handle non-finite values.
Results may differ from the reference program's by a relative error of at most 0.015.
Values may be sent and summed in bfloat16 or wider, within the bound.
A program may use at most 128 MiB of HBM per device.

```python
import math
import jax
import jax.numpy as jnp
from jax import lax

D = 1024
HEADS = 16
HS = 64
FF = 512
TOPK = 4
TOK_DEV = 128
EXPERTS = 64
CAP = 10
TOKENS = 32768
N_HD = 8


def query_key_pair(key):
    base_key = jax.random.fold_in(key, 11)
    query_key, key_key = jax.random.split(base_key, 2)
    query_draw = jnp.clip(1.5 * jax.random.normal(query_key, (TOKENS, D), jnp.float32), -9.0, 9.0)
    key_draw = jnp.clip(1.5 * jax.random.normal(key_key, (TOKENS, D), jnp.float32), -9.0, 9.0)
    return (query_draw, key_draw)


def draw_queries(key, part):
    return query_key_pair(key)[0].astype(jnp.bfloat16)


def draw_keys(key, part):
    return query_key_pair(key)[1].astype(jnp.bfloat16)


def draw_expert_ids(key, part):
    block_count = TOKENS // TOK_DEV
    group_size = EXPERTS // TOPK
    hot_key, cell_key = jax.random.split(jax.random.fold_in(key, 5), 2)
    hot_expert = jax.random.randint(hot_key, (TOPK,), 0, group_size)
    offsets = jnp.arange(group_size - 1, dtype=jnp.int32)

    def one_block(block_key):
        first_key, second_key = jax.random.split(block_key)
        columns = []
        for column in range(TOPK):
            others = (hot_expert[column] + 1 + offsets) % group_size
            cell_list = jax.random.permutation(jax.random.fold_in(first_key, column), jnp.repeat(others, CAP))
            sequence = jnp.concatenate([jnp.full((CAP,), hot_expert[column], jnp.int32), cell_list.astype(jnp.int32)])[:TOK_DEV]
            sequence = jax.random.permutation(jax.random.fold_in(second_key, column), sequence)
            columns.append(sequence + column * group_size)
        return jnp.stack(columns, axis=1)
    block_keys = jax.random.split(cell_key, block_count)
    return jax.vmap(one_block)(block_keys).reshape(TOKENS, TOPK).astype(jnp.int32)


def steps_of(stream_key, shape, pieces, least, top_value):
    level, own = 1.0, jax.random.fold_in(stream_key, 6)
    for axis_at, parts in pieces:
        heights = jnp.exp(jax.random.uniform(jax.random.fold_in(own, axis_at), (parts,), jnp.float32, least / len(pieces), top_value / len(pieces)))
        level = level * jnp.repeat(heights, shape[axis_at] // parts).reshape([-1 if axis == axis_at else 1 for axis in range(len(shape))])
    return level


def normal_values(key, extent, spread, bound, cuts=(), kind=jnp.bfloat16):
    values = spread * jax.random.normal(key, extent, jnp.float32)
    if cuts:
        values = values * steps_of(key, extent, cuts, -0.22, 0.18)
    return jnp.clip(values, -bound, bound).astype(kind)


def setup_inputs(seed: int = 0) -> dict:
    seeds = jax.random.split(jax.random.key(seed), 11)
    return {
        "stream": normal_values(seeds[0], (TOKENS, D), 0.5, 3.0, ((0, 256),)),
        "queries": draw_queries(jax.random.fold_in(seeds[10], 71), 0),
        "keys": draw_keys(jax.random.fold_in(seeds[10], 71), 0),
        "values": normal_values(seeds[3], (TOKENS, D), 1.0, 6.0, ((0, 256),)),
        "out_proj": normal_values(seeds[4], (D, D), (D // 4) ** -0.5, 0.375),
        "norm_gain": jnp.clip(1.0 + 0.1 * jax.random.normal(seeds[5], (D,), jnp.float32), 0.5, 1.5),
        "expert_weights": normal_values(seeds[6], (D, EXPERTS, 3, FF), D ** -0.5, 0.1875, ((1, 32),)),
        "expert_ids": draw_expert_ids(jax.random.fold_in(seeds[10], 71), 0),
        "gate_weights": jnp.clip(jnp.exp(math.log(1.0) - 2.3025851 * jax.random.uniform(seeds[8], (TOKENS, TOPK), jnp.float32) ** steps_of(seeds[8], (TOKENS, TOPK), ((0, 256),), -0.2, 0.2)), 0.1, 1.0),
        "out_cotangent": normal_values(seeds[9], (TOKENS, D), 1.0, 6.0, ((0, 256),)),
    }


NORM_EPS = 1e-06

def silu_parts(pre_gate):
    sigmoid = 1.0 / (1.0 + jnp.exp(-pre_gate))
    return (pre_gate * sigmoid, sigmoid * (1.0 + pre_gate * (1.0 - sigmoid)))

def attend_sequence(query_rows, key_rows, value_rows):
    length = query_rows.shape[0]
    query_heads = query_rows.reshape(length, HEADS, HS).astype(jnp.float32)
    key_heads = key_rows.reshape(length, HEADS, HS).astype(jnp.float32)
    value_heads = value_rows.reshape(length, HEADS, HS).astype(jnp.float32)
    scores = jnp.einsum('qhd,khd->hqk', query_heads, key_heads) * (1.0 / math.sqrt(HS))
    row_max = lax.optimization_barrier(jnp.max(scores, axis=2, keepdims=True))
    raw_weights = jnp.exp(scores - row_max)
    row_total = lax.optimization_barrier(jnp.sum(raw_weights, axis=2))
    rounded = raw_weights.astype(jnp.bfloat16).astype(jnp.float32)
    mixed_heads = jnp.einsum('hqk,khd->qhd', rounded, value_heads)
    result = mixed_heads / jnp.transpose(row_total)[:, :, None]
    return result.astype(jnp.bfloat16).reshape(length, HEADS * HS)

def expert_reference(cell_inputs, cell_cots, weight_block):
    gate_up = weight_block[:, :2].astype(jnp.float32)
    down_t = weight_block[:, 2].astype(jnp.float32)
    pre_pair = jnp.einsum('md,dcf->mcf', cell_inputs.astype(jnp.float32), gate_up)
    activated, act_slope = silu_parts(pre_pair[:, 0])
    up_value = pre_pair[:, 1]
    hidden = (activated * up_value).astype(jnp.bfloat16)
    expert_outs = jnp.einsum('mf,df->md', hidden.astype(jnp.float32), down_t).astype(jnp.bfloat16)
    back_hidden = jnp.einsum('md,df->mf', cell_cots.astype(jnp.float32), down_t)
    hidden_grads = jnp.stack([back_hidden * up_value * act_slope, back_hidden * activated], axis=1).astype(jnp.bfloat16)
    expert_grads = jnp.einsum('mcf,dcf->md', hidden_grads.astype(jnp.float32), gate_up).astype(jnp.bfloat16)
    return (expert_outs, expert_grads)

def reference(stream, queries, keys, values, out_proj, norm_gain, expert_weights, expert_ids, gate_weights, out_cotangent):
    length = TOK_DEV * N_HD
    seq_count = TOKENS // length

    def one_sequence(seq_index):
        row_start = seq_index * length
        return attend_sequence(lax.dynamic_slice_in_dim(queries, row_start, length, 0), lax.dynamic_slice_in_dim(keys, row_start, length, 0), lax.dynamic_slice_in_dim(values, row_start, length, 0))
    attended = lax.map(one_sequence, jnp.arange(seq_count, dtype=jnp.int32)).reshape(TOKENS, D)
    projected = jnp.dot(attended, out_proj, preferred_element_type=jnp.float32)
    mix_stream = (stream.astype(jnp.float32) + projected).astype(jnp.bfloat16)
    stream_wide = mix_stream.astype(jnp.float32)
    inverse = lax.rsqrt(lax.optimization_barrier(jnp.mean(stream_wide * stream_wide, axis=1, keepdims=True)) + NORM_EPS)
    normed = (norm_gain * stream_wide * inverse).astype(jnp.bfloat16)
    block_count = TOKENS // TOK_DEV
    block_ids = expert_ids.reshape(block_count, TOK_DEV * TOPK)
    onehot = (block_ids[:, :, None] == jnp.arange(EXPERTS, dtype=jnp.int32)[None, None, :]).astype(jnp.int32)
    slot_index = lax.optimization_barrier(jnp.sum((jnp.cumsum(onehot, axis=1) - onehot) * onehot, axis=2))
    block_index = jnp.arange(block_count, dtype=jnp.int32)[:, None]
    position = (block_index * CAP + slot_index).reshape(-1).astype(jnp.int32)
    flat_ids = expert_ids.reshape(-1).astype(jnp.int32)
    token_index = jnp.arange(TOKENS * TOPK, dtype=jnp.int32) // TOPK
    source = jnp.full((EXPERTS, block_count * CAP), TOKENS, jnp.int32).at[flat_ids, position].set(token_index)
    gate_table = jnp.zeros((EXPERTS, block_count * CAP), jnp.float32).at[flat_ids, position].set(gate_weights.reshape(-1))
    normed_pad = jnp.concatenate([normed, jnp.zeros((1, D), jnp.bfloat16)], axis=0)
    cot_pad = jnp.concatenate([out_cotangent, jnp.zeros((1, D), jnp.bfloat16)], axis=0)
    weights_major = jnp.moveaxis(expert_weights, 1, 0)

    def expert_step(running, expert_item):
        out_accum, grad_accum = running
        cell_rows, gate_column, weight_block = expert_item
        expert_outs, expert_grads = expert_reference(jnp.take(normed_pad, cell_rows, axis=0), jnp.take(cot_pad, cell_rows, axis=0), weight_block)
        out_accum = out_accum.at[cell_rows].add(gate_column[:, None] * expert_outs.astype(jnp.float32))
        grad_accum = grad_accum.at[cell_rows].add(gate_column[:, None] * expert_grads.astype(jnp.float32))
        return ((out_accum, grad_accum), None)
    start_state = (jnp.zeros((TOKENS + 1, D), jnp.float32), jnp.zeros((TOKENS + 1, D), jnp.float32))
    (out_accum, grad_accum), _ = lax.scan(expert_step, start_state, (source, gate_table, weights_major))
    block_out = (stream_wide + out_accum[:TOKENS]).astype(jnp.bfloat16)
    weighted = norm_gain * grad_accum[:TOKENS]
    scaled = stream_wide * inverse
    stream_grad = out_cotangent.astype(jnp.float32) + inverse * (weighted - scaled * lax.optimization_barrier(jnp.mean(weighted * scaled, axis=1, keepdims=True)))
    return (block_out, stream_grad.astype(jnp.bfloat16))
```

```python
import functools
import math

import jax
import jax.numpy as jnp
from jax import lax
from jax.experimental import pallas as pl
from jax.experimental.pallas import tpu as pltpu
from jax.sharding import PartitionSpec as P

HS = 64
NORM_EPS = 1e-06
NY = 4
PADDED = 32
BF = jnp.bfloat16
F32 = jnp.float32
MESH = pl.DeviceIdType.MESH


def ring_chunks(planes):
    order = [0]
    for step in range(1, planes // 2):
        order += [step, planes - step]
    order.append(planes // 2)
    return [order[at : at + 3] for at in range(0, planes, 3)]


def moe_kernel(
    planes,
    cap,
    info_ref,
    rows_ref,
    cot_ref,
    mix_ref,
    inverse_ref,
    gain_ref,
    weights_ref,
    out_ref,
    grad_ref,
    info_all,
    gathered,
    slot_send,
    slot_recv,
    expert_send,
    expert_recv,
    weights,
    back_hidden,
    hidden,
    hidden_grads,
    sum_send,
    sum_recv,
    info_sems,
    gather_send_sems,
    gather_recv_sems,
    slot_sems,
    slot_local_sems,
    expert_sems,
    expert_local_sems,
    sum_send_sems,
    sum_recv_sems,
    weight_sem,
):
    tokens, width = rows_ref.shape
    local_count = weights.shape[0]
    inner = weights.shape[2] // 3
    half = planes // 2
    half_tokens = tokens // 2
    half_width = width // 2
    tile = min(256, half_width)
    chunks = ring_chunks(planes)
    place = {offset: (c, q) for c, chunk in enumerate(chunks) for q, offset in enumerate(chunk)}
    chunk_rows = NY * local_count * PADDED

    me = lax.axis_index("rcv")
    plane = me // NY
    row = lax.rem(me, NY)
    ring = (
        lax.rem(plane + 1, planes) * NY + row,
        lax.rem(plane + planes - 1, planes) * NY + row,
    )
    mates = [lax.rem(row + step, NY) for step in range(1, NY)]

    weight_copy = pltpu.make_async_copy(weights_ref, weights, weight_sem)
    weight_copy.start()

    barrier = pltpu.get_barrier_semaphore()
    for target in ring:
        pl.semaphore_signal(barrier, inc=1, device_id={"rcv": target}, device_id_type=MESH)
    for mate in mates:
        pl.semaphore_signal(
            barrier, inc=1, device_id={"rcv": plane * NY + mate}, device_id_type=MESH
        )
    pl.semaphore_wait(barrier, 2 + len(mates))

    def slot_of(array, offset):
        if offset == 0:
            return (rows_ref, cot_ref)[array]
        return gathered.at[array, offset]

    def ring_offsets(direction, step):
        if direction == 0:
            return step - 1, step
        return (planes - step + 1) % planes, planes - step

    def gather_copy(array, direction, step, piece):
        source, target = ring_offsets(direction, step)
        part = pl.ds(piece * half_tokens, half_tokens)
        return pltpu.make_async_remote_copy(
            src_ref=slot_of(array, source).at[part],
            dst_ref=gathered.at[array, target].at[part],
            send_sem=gather_send_sems.at[array, direction, step - 1, piece],
            recv_sem=gather_recv_sems.at[array, direction, step - 1, piece],
            device_id={"rcv": ring[direction]},
            device_id_type=MESH,
        )

    def info_copy(direction, step):
        source, target = ring_offsets(direction, step)
        return pltpu.make_async_remote_copy(
            src_ref=info_ref if source == 0 else info_all.at[source],
            dst_ref=info_all.at[target],
            send_sem=info_sems.at[0, direction, step - 1],
            recv_sem=info_sems.at[1, direction, step - 1],
            device_id={"rcv": ring[direction]},
            device_id_type=MESH,
        )

    def info_of(offset):
        return info_ref[...] if offset == 0 else info_all[offset]

    def slot_mask(position, cells):
        index = lax.broadcasted_iota(jnp.int32, (chunk_rows, tokens), 0)
        expert = lax.shift_right_logical(index, 5)
        inside = lax.bitwise_and(index, 31) - cap * position
        cell = (plane * (NY * local_count) + expert) * cap + inside
        cell = jnp.where((inside >= 0) & (inside < cap), cell, -1).astype(F32)
        return [cell == cells[k : k + 1, :] for k in range(4)]

    def one_hot(offset):
        info = info_of(offset)
        hits = slot_mask(place[offset][1], info)
        total = jnp.zeros((chunk_rows, tokens), F32)
        for hit in hits:
            total = jnp.where(hit, 1.0, total)
        return total.astype(BF)

    def gate_map(offset):
        info = info_of(offset)
        hits = slot_mask(place[offset][1], info)
        total = jnp.zeros((chunk_rows, tokens), F32)
        for k, hit in enumerate(hits):
            total = jnp.where(hit, info[4 + k : 5 + k, :], total)
        high = total.astype(BF)
        return high, (total - high.astype(F32)).astype(BF)

    def slot_copy(array, c, step):
        mate = mates[step - 1]
        return pltpu.make_async_remote_copy(
            src_ref=slot_send.at[array, c, mate],
            dst_ref=slot_recv.at[array, :, c, row],
            send_sem=slot_sems.at[0, array, c, step - 1],
            recv_sem=slot_sems.at[1, array, c, step - 1],
            device_id={"rcv": plane * NY + mate},
            device_id_type=MESH,
        )

    def slot_local_copy(array, c):
        return pltpu.make_async_copy(
            slot_send.at[array, c, row],
            slot_recv.at[array, :, c, row],
            slot_local_sems.at[array, c],
        )

    def pack(array, c):
        maps = [one_hot(offset) for offset in chunks[c]]
        for at in range(0, width, tile):
            columns = pl.ds(at, tile)
            total = None
            for selector, offset in zip(maps, chunks[c]):
                term = jnp.dot(
                    selector, slot_of(array, offset)[:, columns], preferred_element_type=F32
                )
                total = term if total is None else total + term
            slot_send[array, c, :, :, :, columns] = total.astype(BF).reshape(
                NY, local_count, PADDED, tile
            )
        for step in range(1, NY):
            slot_copy(array, c, step).start()
        slot_local_copy(array, c).start()

    def gather_and_pack(array):
        ready = {0}
        done = 0
        for step in range(1, half + 1):
            for turn in range(2):
                for direction in range(2):
                    piece = direction if turn == 0 else 1 - direction
                    if step == half and turn == 1:
                        continue
                    gather_copy(array, direction, step, piece).wait_recv()
                    if step < half - 1 or (step == half - 1 and piece == direction):
                        gather_copy(array, direction, step + 1, piece).start()
            ready |= {step, planes - step}
            while done < len(chunks) and set(chunks[done]) <= ready:
                pack(array, done)
                done += 1

    for direction in range(2):
        info_copy(direction, 1).start()
    for array in (1, 0):
        for turn in range(2):
            for direction in range(2):
                gather_copy(array, direction, 1, direction if turn == 0 else 1 - direction).start()
    for step in range(1, half + 1):
        for direction in range(2):
            if step == half and direction == 1:
                continue
            info_copy(direction, step).wait_recv()
            if step < half - 1 or (step == half - 1 and direction == 0):
                info_copy(direction, step + 1).start()

    def wait_slots(array):
        for c in range(len(chunks)):
            for step in range(1, NY):
                slot_copy(array, c, step).wait_recv()
            slot_local_copy(array, c).wait()

    gather_and_pack(1)
    gather_and_pack(0)
    weight_copy.wait()
    expert_rows = len(chunks) * NY * PADDED
    inner_tile = min(256, inner)

    wait_slots(1)
    for e in range(local_count):
        cot_rows = slot_recv[1, e].reshape(expert_rows, width)
        for at in range(0, inner, inner_tile):
            back_hidden[e, :, at : at + inner_tile] = jnp.dot(
                cot_rows,
                weights[e, :, 2 * inner + at : 2 * inner + at + inner_tile],
                preferred_element_type=F32,
            )

    def expert_copy(array, c, step):
        mate = mates[step - 1]
        return pltpu.make_async_remote_copy(
            src_ref=expert_send.at[array, :, c, mate],
            dst_ref=expert_recv.at[array, c, row],
            send_sem=expert_sems.at[0, array, c, step - 1],
            recv_sem=expert_sems.at[1, array, c, step - 1],
            device_id={"rcv": plane * NY + mate},
            device_id_type=MESH,
        )

    def expert_local_copy(array, c):
        return pltpu.make_async_copy(
            expert_send.at[array, :, c, row],
            expert_recv.at[array, c, row],
            expert_local_sems.at[array, c],
        )

    def send_experts(array):
        for c in reversed(range(len(chunks))):
            for step in range(1, NY):
                expert_copy(array, c, step).start()
            expert_local_copy(array, c).start()

    contract_last = (((1,), (1,)), ((), ()))
    wait_slots(0)
    for e in range(local_count):
        row_values = slot_recv[0, e].reshape(expert_rows, width)
        for at in range(0, inner, inner_tile):
            gate = jnp.dot(
                row_values, weights[e, :, at : at + inner_tile], preferred_element_type=F32
            )
            up = jnp.dot(
                row_values,
                weights[e, :, inner + at : inner + at + inner_tile],
                preferred_element_type=F32,
            )
            sigmoid = 1.0 / (1.0 + jnp.exp(-gate))
            active = gate * sigmoid
            slope = sigmoid * (1.0 + gate * (1.0 - sigmoid))
            hidden[e, :, at : at + inner_tile] = (active * up).astype(BF)
            back = back_hidden[e, :, at : at + inner_tile]
            hidden_grads[e, :, at : at + inner_tile] = (back * up * slope).astype(BF)
            hidden_grads[e, :, inner + at : inner + at + inner_tile] = (back * active).astype(BF)
        for at in range(0, width, tile):
            result = lax.dot_general(
                hidden[e],
                weights[e, at : at + tile, 2 * inner : 3 * inner],
                contract_last,
                preferred_element_type=F32,
            )
            expert_send[0, e, :, :, :, at : at + tile] = result.astype(BF).reshape(
                len(chunks), NY, PADDED, tile
            )
    send_experts(0)
    for e in range(local_count):
        for at in range(0, width, tile):
            result = lax.dot_general(
                hidden_grads[e],
                weights[e, at : at + tile, 0 : 2 * inner],
                contract_last,
                preferred_element_type=F32,
            )
            expert_send[1, e, :, :, :, at : at + tile] = result.astype(BF).reshape(
                len(chunks), NY, PADDED, tile
            )
    send_experts(1)

    contract_first = (((0,), (0,)), ((), ()))

    def partial(array, offset, maps, at):
        c = place[offset][0]
        block = expert_recv[array, c, :, :, :, at : at + tile].reshape(chunk_rows, tile)
        return lax.dot_general(
            maps[0], block, contract_first, preferred_element_type=F32
        ) + lax.dot_general(maps[1], block, contract_first, preferred_element_type=F32)

    def sum_copy(array, direction, step, piece):
        part = pl.ds(piece * half_width, half_width)
        return pltpu.make_async_remote_copy(
            src_ref=sum_send.at[array, direction, step - 1, :, part],
            dst_ref=sum_recv.at[array, direction, step - 1, :, part],
            send_sem=sum_send_sems.at[array, direction, step - 1, piece],
            recv_sem=sum_recv_sems.at[array, direction, step - 1, piece],
            device_id={"rcv": ring[direction]},
            device_id_type=MESH,
        )

    arrived = set()

    def wait_experts(array, c):
        if (array, c) in arrived:
            return
        arrived.add((array, c))
        for step in range(1, NY):
            expert_copy(array, c, step).wait_recv()
        expert_local_copy(array, c).wait()

    def home_offset(direction, step):
        distance = half - step + 1
        return planes - distance if direction == 0 else distance

    def sum_step(array, direction, step):
        offset = home_offset(direction, step)
        wait_experts(array, place[offset][0])
        maps = gate_map(offset)
        pieces = (direction,) if step == 1 else (direction, 1 - direction)
        for piece in pieces:
            added = step > 2 or (step == 2 and piece == direction)
            if added:
                sum_copy(array, direction, step - 1, piece).wait_recv()
            for at in range(piece * half_width, (piece + 1) * half_width, tile):
                total = partial(array, offset, maps, at)
                if added:
                    total = total + sum_recv[
                        array, direction, step - 2, :, at : at + tile
                    ].astype(F32)
                sum_send[array, direction, step - 1, :, at : at + tile] = total.astype(BF)
            sum_copy(array, direction, step, piece).start()

    for step in range(1, half + 1):
        for array in range(2):
            for direction in range(2):
                sum_step(array, direction, step)

    maps = gate_map(0)

    def final_sum(array):
        wait_experts(array, place[0][0])
        terms = [partial(array, 0, maps, at) for at in range(0, width, tile)]
        total = jnp.concatenate(terms, axis=1)
        for direction in range(2):
            for piece in range(2):
                sum_copy(array, direction, half, piece).wait_recv()
        for direction in range(2):
            total = total + sum_recv[array, direction, half - 1].astype(F32)
        return total

    wide = mix_ref[...].astype(F32)
    out_ref[...] = (wide + final_sum(0)).astype(BF)
    weighted = gain_ref[...] * final_sum(1)
    inverse = inverse_ref[...]
    scaled = wide * inverse
    mean = jnp.mean(weighted * scaled, axis=1, keepdims=True)
    grad_ref[...] = (cot_ref[...].astype(F32) + inverse * (weighted - scaled * mean)).astype(BF)

    for direction in range(2):
        for step in range(1, half + 1):
            if step < half or direction == 0:
                info_copy(direction, step).wait_send()
            for array in range(2):
                for piece in range(2):
                    if step < half or piece == direction:
                        gather_copy(array, direction, step, piece).wait_send()
                    if step > 1 or piece == direction:
                        sum_copy(array, direction, step, piece).wait_send()
    for array in range(2):
        for c in range(len(chunks)):
            for step in range(1, NY):
                slot_copy(array, c, step).wait_send()
                expert_copy(array, c, step).wait_send()


def moe(info, rows, cot, mix, inverse, gain, weights, cap):
    planes = lax.axis_size("rcv") // NY
    tokens, width = rows.shape
    local_count, _, wide_inner = weights.shape
    inner = wide_inner // 3
    half = planes // 2
    chunk_count = len(ring_chunks(planes))
    vmem = pl.BlockSpec(memory_space=pltpu.VMEM)
    dma = pltpu.SemaphoreType.DMA
    expert_rows = chunk_count * NY * PADDED
    return pl.pallas_call(
        functools.partial(moe_kernel, planes, cap),
        out_shape=(
            jax.ShapeDtypeStruct((tokens, width), BF),
            jax.ShapeDtypeStruct((tokens, width), BF),
        ),
        in_specs=[vmem] * 6 + [pl.BlockSpec(memory_space=pl.ANY)],
        out_specs=(vmem, vmem),
        scratch_shapes=[
            pltpu.VMEM((planes, 8, tokens), F32),
            pltpu.VMEM((2, planes, tokens, width), BF),
            pltpu.VMEM((2, chunk_count, NY, local_count, PADDED, width), BF),
            pltpu.VMEM((2, local_count, chunk_count, NY, PADDED, width), BF),
            pltpu.VMEM((2, local_count, chunk_count, NY, PADDED, width), BF),
            pltpu.VMEM((2, chunk_count, NY, local_count, PADDED, width), BF),
            pltpu.VMEM(weights.shape, BF),
            pltpu.VMEM((local_count, expert_rows, inner), F32),
            pltpu.VMEM((local_count, expert_rows, inner), BF),
            pltpu.VMEM((local_count, expert_rows, 2 * inner), BF),
            pltpu.VMEM((2, 2, half, tokens, width), BF),
            pltpu.VMEM((2, 2, half, tokens, width), BF),
            dma((2, 2, half)),
            dma((2, 2, half, 2)),
            dma((2, 2, half, 2)),
            dma((2, 2, chunk_count, NY - 1)),
            dma((2, chunk_count)),
            dma((2, 2, chunk_count, NY - 1)),
            dma((2, chunk_count)),
            dma((2, 2, half, 2)),
            dma((2, 2, half, 2)),
            dma(()),
        ],
        compiler_params=pltpu.CompilerParams(
            collective_id=1, has_side_effects=True, vmem_limit_bytes=60 * 1024 * 1024
        ),
        name="moe",
    )(info, rows, cot, mix, inverse, gain, weights)


def routing_info(expert_ids, gate_weights, cap):
    rows = expert_ids.shape[0]
    ids = expert_ids.T
    earlier = jnp.arange(rows)[None, :] < jnp.arange(rows)[:, None]
    same = (ids[:, :, None] == ids[:, None, :]) & earlier[None]
    slot = jnp.sum(same.astype(F32), axis=2)
    cell = ids.astype(F32) * cap + slot
    return jnp.concatenate([cell, gate_weights.T], axis=0)


def per_device(
    stream,
    queries,
    keys,
    values,
    out_proj,
    norm_gain,
    expert_weights,
    expert_ids,
    gate_weights,
    out_cotangent,
):
    row_count, feature_width = stream.shape
    groups = lax.axis_size("rcv")
    local_count = expert_weights.shape[1]
    experts = local_count * groups
    top_count = expert_ids.shape[1]
    cap = (5 * row_count * top_count + 4 * experts - 1) // (4 * experts)
    score_scale = 1.0 / math.sqrt(HS)
    info = routing_info(expert_ids, gate_weights, cap)
    inner = expert_weights.shape[3]
    weights = jnp.transpose(expert_weights, (1, 0, 2, 3)).reshape(
        local_count, feature_width, 3 * inner
    )

    query_all, key_all, value_all = (
        lax.all_to_all(queries, "hd", split_axis=1, concat_axis=0, tiled=True),
        lax.all_to_all(keys, "hd", split_axis=1, concat_axis=0, tiled=True),
        lax.all_to_all(values, "hd", split_axis=1, concat_axis=0, tiled=True),
    )
    length = query_all.shape[0]
    head_count = query_all.shape[1] // HS
    block_rows = math.gcd(length, 512)
    key_heads = key_all.reshape(length, head_count, HS)
    value_heads = value_all.reshape(length, head_count, HS)

    def one_block(row_start):
        query_block = lax.dynamic_slice_in_dim(query_all, row_start, block_rows, 0).reshape(
            block_rows, head_count, HS
        )
        scores = (
            jnp.einsum("qhd,khd->hqk", query_block, key_heads, preferred_element_type=F32)
            * score_scale
        )
        row_max = jnp.max(scores, axis=2, keepdims=True)
        raw_weights = jnp.exp(scores - row_max)
        row_total = jnp.sum(raw_weights, axis=2)
        mixed_heads = jnp.einsum(
            "hqk,khd->qhd", raw_weights.astype(BF), value_heads, preferred_element_type=F32
        )
        result = mixed_heads / jnp.transpose(row_total)[:, :, None]
        return result.astype(BF).reshape(block_rows, head_count * HS)

    starts = jnp.arange(length // block_rows, dtype=jnp.int32) * block_rows
    head_result = lax.map(one_block, starts).reshape(length, head_count * HS)
    attended = lax.all_to_all(head_result, "hd", split_axis=0, concat_axis=1, tiled=True)
    projected = jnp.dot(attended, out_proj, preferred_element_type=F32)
    mix_stream = (stream.astype(F32) + projected).astype(BF)
    stream_wide = mix_stream.astype(F32)
    inverse = lax.rsqrt(jnp.mean(stream_wide * stream_wide, axis=1, keepdims=True) + NORM_EPS)
    normed = (norm_gain * stream_wide * inverse).astype(BF)
    return moe(
        info, normed, out_cotangent, mix_stream, inverse, norm_gain[None, :], weights, cap
    )


def solution(mesh):
    split = P(("rcv", "hd"), None)
    placed = (split,) * 4 + (P(), P(), P(None, "rcv", None, None)) + (split,) * 3
    return jax.shard_map(
        per_device, mesh=mesh, in_specs=placed, out_specs=(split, split), check_vma=False
    )
```
